512 devices in a mesh: row: 32 (over z, y_hi), col: 16 (over y_lo, x, core).
Axes of the slice: x: 4, y: 8 (y_hi: 4, y_lo: 2; y = y_hi * 2 + y_lo), z: 8, core: 2. Of those that a mesh axis runs over, the one named last changes fastest.
Arguments:
- signal: float32 [32, 65536], P(None, 'row'), may hold values from -8 to 8
- tile_values: bfloat16 [32, 16, 64, 128, 128], P('row', 'col'), may hold values from 1e-12 to 1, as said below
- tile_places: int32 [32, 16, 2, 64], P('row', 'col'), may hold values from 0 to 31, as said below
- tile_counts: int32 [32, 16], P('row', 'col'), may hold values from 16 to 64, as said below
Outputs:
- first_wavelet: float32 [32, 65536], P(None, 'row')
- second_wavelet: float32 [32, 65536], P(None, 'row')
- lowpass: float32 [32, 65536], P(None, 'row')
The draws below stay inside these ranges and needn't reach their ends.
Inputs may be any that keep to these rules, and one draw needn't show every extreme that they name: `tile_values`: A is symmetric, and every node's row of A has a positive entry on the diagonal. Slots at or after a device's count hold tiles that are not part of A. `tile_places`: place 0 lies below 16, place 1 below 32; the live slots of one device name distinct places. `tile_counts`: some device is full in every draw.
All inputs are finite; a program needn't handle non-finite values.
Results may differ from the reference program's by a relative error of at most 0.0003.
Values may be sent and summed in bfloat16 or wider, within the bound.
No kernel may reach another device: no remote copies, remote signals or barrier semaphores. Data moves between devices by JAX's collectives and lax.ppermute only.
A program may use at most 64 MiB of HBM per device.

```python
import math
import jax
import jax.numpy as jnp
from jax import lax

CH = 32
TILE = 128
NODES = 65536
TILE_ROWS = 16
SQUARE_TILES = 32
K_SLOTS = 64
N_ROW = 32
N_COL = 16


def square_list(base, first, second):
    cells = TILE_ROWS * TILE_ROWS
    grid = jnp.arange(cells, dtype=jnp.int32)
    cell_row = grid // TILE_ROWS
    cell_col = grid % TILE_ROWS
    along = jnp.arange(TILE_ROWS, dtype=jnp.int32)
    low = jnp.minimum(first, second)
    high = jnp.maximum(first, second)
    pair_id = low * N_ROW + high
    order = jax.random.permutation(jax.random.fold_in(base, pair_id), cells).astype(jnp.int32)
    perm_row = cell_row[order]
    perm_col = cell_col[order]
    score = jnp.where(perm_row < perm_col, 0, cells) + grid
    pick = jnp.argsort(score)[:TILE_ROWS // 2]
    upper_row = perm_row[pick]
    upper_col = perm_col[pick]
    diag_row = jnp.concatenate([along, upper_row, upper_col])
    diag_col = jnp.concatenate([along, upper_col, upper_row])
    drawn_row = perm_row[:SQUARE_TILES]
    drawn_col = perm_col[:SQUARE_TILES]
    flip = first > second
    off_row = jnp.where(flip, drawn_col, drawn_row)
    off_col = jnp.where(flip, drawn_row, drawn_col)
    same = first == second
    list_row = jnp.where(same, diag_row, off_row)
    list_col = jnp.where(same, diag_col, off_col)
    gap = jnp.minimum((first - second) % N_ROW, (second - first) % N_ROW)
    extra = jax.random.randint(jax.random.fold_in(base, pair_id + 7 * N_ROW * N_ROW), (), 0, TILE_ROWS // 2 + 1).astype(jnp.int32)
    live_number = jnp.where(gap <= 1, SQUARE_TILES, TILE_ROWS // 2 + extra)
    return (list_row, list_col, live_number)


def device_layout(base, row_block, col_block):
    rows_a, cols_a, count_a = square_list(base, row_block, 2 * col_block)
    rows_b, cols_b, count_b = square_list(base, row_block, 2 * col_block + 1)
    position = jnp.arange(SQUARE_TILES, dtype=jnp.int32)
    live_slot = jnp.concatenate([position < count_a, position < count_b])
    slot_row = jnp.concatenate([rows_a, rows_b])
    slot_col = jnp.concatenate([cols_a, cols_b + TILE_ROWS])
    squares = jnp.concatenate([jnp.full((SQUARE_TILES,), 2 * col_block, jnp.int32), jnp.full((SQUARE_TILES,), 2 * col_block + 1, jnp.int32)])
    order = jnp.argsort(jnp.where(live_slot, 0, K_SLOTS) + jnp.arange(K_SLOTS, dtype=jnp.int32))
    return (slot_row[order], slot_col[order], squares[order], count_a + count_b)


def graph_layouts(key):
    base = jax.random.fold_in(key, 11)
    device_ids = jnp.arange(N_ROW * N_COL, dtype=jnp.int32)

    def one_device(index):
        slot_row, slot_col, squares, count = device_layout(base, index // N_COL, index % N_COL)
        return (jnp.stack([slot_row, slot_col]), count)
    places, counts = lax.map(one_device, device_ids)
    return (places.reshape(N_ROW, N_COL, 2, K_SLOTS), counts.reshape(N_ROW, N_COL))


def draw_tile_places(key, part):
    return graph_layouts(jax.random.fold_in(key, 5))[0]


def draw_tile_counts(key, part):
    return graph_layouts(jax.random.fold_in(key, 5))[1]


def draw_tile_values(key, part):
    graph_key = jax.random.fold_in(key, 5)
    base = jax.random.fold_in(graph_key, 11)
    value_key = jax.random.fold_in(graph_key, 29)
    total_tiles = N_ROW * TILE_ROWS
    inner = jnp.arange(TILE, dtype=jnp.int32)
    lower_half = inner[:, None] <= inner[None, :]

    def one_tile(global_row, global_col):
        pair = jnp.minimum(global_row, global_col) * total_tiles + jnp.maximum(global_row, global_col)
        raw = jnp.exp(jax.random.uniform(jax.random.fold_in(value_key, pair), (TILE, TILE), jnp.float32, math.log(1e-12), 0.0))
        symmetric = jnp.where(lower_half, raw, raw.T)
        picked = jnp.where(global_row < global_col, raw, jnp.where(global_row > global_col, raw.T, symmetric))
        return picked.astype(jnp.bfloat16)

    def one_device(index):
        row_block = index // N_COL
        col_block = index % N_COL
        slot_row, slot_col, squares, count = device_layout(base, row_block, col_block)
        global_row = row_block * TILE_ROWS + slot_row
        global_col = squares * TILE_ROWS + slot_col % TILE_ROWS
        return jax.vmap(one_tile)(global_row, global_col)
    values = lax.map(one_device, jnp.arange(N_ROW * N_COL, dtype=jnp.int32))
    return values.reshape(N_ROW, N_COL, K_SLOTS, TILE, TILE)


def draw_signal(key, part):
    key_rough = jax.random.fold_in(key, 0)
    rough = jax.random.normal(key_rough, (CH, NODES), jnp.float32) * 1.5
    return jnp.clip(rough, -8.0, 8.0)


def setup_inputs(seed: int = 0) -> dict:
    splits = jax.random.split(jax.random.key(seed), 5)
    signal = draw_signal(jax.random.fold_in(splits[4], 71), 0)
    tile_values = draw_tile_values(jax.random.fold_in(splits[4], 71), 0)
    tile_places = draw_tile_places(jax.random.fold_in(splits[4], 71), 0)
    tile_counts = draw_tile_counts(jax.random.fold_in(splits[4], 71), 0)
    return {"signal": signal, "tile_values": tile_values, "tile_places": tile_places, "tile_counts": tile_counts}


highest_precision = lax.Precision.HIGHEST


def reference(signal, tile_values, tile_places, tile_counts):
    halves = N_ROW // N_COL
    row_len = TILE_ROWS * TILE
    col_len = halves * row_len
    slot_ids = jnp.arange(K_SLOTS, dtype=jnp.int32)
    row_ids = jnp.arange(TILE_ROWS, dtype=jnp.int32)

    def live_rows(row_block, col_block):
        live_slot = (slot_ids < tile_counts[row_block, col_block]).astype(jnp.float32)
        places = tile_places[row_block, col_block]
        return (places[0][:, None] == row_ids[None, :]).astype(jnp.float32) * live_slot[:, None]

    def block_degree(row_block):
        def per_col(running, col_block):
            sums = jnp.sum(tile_values[row_block, col_block].astype(jnp.float32), axis=2)
            row_hot = live_rows(row_block, col_block)
            return running + jnp.einsum("kt,ka->ta", row_hot, sums, precision=highest_precision), None
        running, _ = lax.scan(per_col, jnp.zeros((TILE_ROWS, TILE), jnp.float32), jnp.arange(N_COL, dtype=jnp.int32))
        return running.reshape(row_len)

    degree = lax.map(block_degree, jnp.arange(N_ROW, dtype=jnp.int32)).reshape(NODES)

    def walk(vector):
        rounded = (vector / degree[None, :]).astype(jnp.bfloat16)
        scaled = lax.optimization_barrier(rounded).astype(jnp.float32)

        def block_apply(row_block):
            def per_col(running, col_block):
                column = lax.dynamic_slice_in_dim(scaled, col_block * col_len, col_len, 1)
                column = column.reshape(CH, halves * TILE_ROWS, TILE)
                picked = jnp.take(column, tile_places[row_block, col_block, 1], axis=1)
                blocks = tile_values[row_block, col_block].astype(jnp.float32)
                products = jnp.einsum("kab,ckb->cka", blocks, picked, precision=highest_precision)
                row_hot = live_rows(row_block, col_block)
                return running + jnp.einsum("cka,kt->cta", products, row_hot, precision=highest_precision), None
            running, _ = lax.scan(per_col, jnp.zeros((CH, TILE_ROWS, TILE), jnp.float32), jnp.arange(N_COL, dtype=jnp.int32))
            return running.reshape(CH, row_len)

        row_parts = lax.map(block_apply, jnp.arange(N_ROW, dtype=jnp.int32))
        spread = jnp.transpose(row_parts, (1, 0, 2)).reshape(CH, NODES)
        return 0.5 * (vector + spread)

    walked = walk(signal)
    lowpass = walk(walked)
    return jnp.abs(signal - walked), jnp.abs(walked - lowpass), lowpass
```

```python
import jax
import jax.numpy as jnp
from jax import lax
from jax.sharding import PartitionSpec as P

highest_precision = lax.Precision.HIGHEST


def column_perms(row_size, col_size):
    halves = row_size // col_size

    def flat(r, c):
        return r * col_size + c

    perms = []
    for shift in range(halves):
        pairs = []
        for c in range(col_size):
            for j in range(halves):
                for m in range(row_size // halves):
                    pairs.append((flat(halves * c + j, m), flat(halves * m + (j + shift) % halves, c)))
        perms.append(pairs)
    return perms


def on_device(signal, tile_values, tile_places, tile_counts):
    channels, row_len = signal.shape
    slot_count = tile_values.shape[2]
    tile_width = tile_values.shape[3]
    tile_rows = row_len // tile_width
    row_size = lax.axis_size("row")
    col_size = lax.axis_size("col")
    halves = row_size // col_size
    blocks = tile_values.reshape(slot_count, tile_width, tile_width)
    places = tile_places.reshape(2, slot_count)
    live_count = tile_counts.reshape(())
    live_slot = (lax.iota(jnp.int32, slot_count) < live_count).astype(jnp.float32)
    row_hot = (places[0][:, None] == lax.iota(jnp.int32, tile_rows)[None, :]).astype(
        jnp.float32
    ) * live_slot[:, None]
    perms = column_perms(row_size, col_size)
    parity = lax.axis_index("row") % halves
    col_tile = ((parity - places[1] // tile_rows) % halves) * tile_rows + places[1] % tile_rows

    sums = jnp.sum(blocks, axis=2, dtype=jnp.float32)
    degree_part = jnp.einsum("kt,ka->ta", row_hot, sums, precision=highest_precision)
    degree = lax.psum(degree_part.reshape(row_len), "col")

    def walk(vector):
        scaled = (vector / degree[None, :]).astype(jnp.bfloat16)
        pieces = [lax.ppermute(scaled, ("row", "col"), perm) for perm in perms]
        column = jnp.concatenate(pieces, axis=1).reshape(channels, halves * tile_rows, tile_width)
        picked = jnp.take(column, col_tile, axis=1)
        products = jnp.einsum(
            "kab,ckb->cka", blocks, picked, preferred_element_type=jnp.float32
        )
        partial_value = jnp.einsum("cka,kt->cta", products, row_hot, precision=highest_precision)
        spread = lax.psum(partial_value.reshape(channels, row_len), "col")
        return 0.5 * (vector + spread)

    walked = walk(signal)
    lowpass = walk(walked)
    return (jnp.abs(signal - walked), jnp.abs(walked - lowpass), lowpass)


def solution(mesh):
    in_specs = (
        P(None, "row"),
        P("row", "col", None, None, None),
        P("row", "col", None, None),
        P("row", "col"),
    )
    out_specs = (P(None, "row"), P(None, "row"), P(None, "row"))
    return jax.shard_map(
        on_device, mesh=mesh, in_specs=in_specs, out_specs=out_specs, check_vma=False
    )
```
